512 devices in a mesh: tm: 32 (over z_hi, y, core), space: 16 (over x, z_lo).
Axes of the slice: x: 4, y: 8, z: 8 (z_hi: 2, z_lo: 4; z = z_hi * 4 + z_lo), core: 2. Of those that a mesh axis runs over, the one named last changes fastest.
Arguments:
- state: float32 [1024, 384, 128], P('tm', 'space'), may hold values from -6 to 6
- forcing: float32 [1024, 384, 128], P('tm', 'space'), may hold values from -6 to 6
- initial: float32 [384, 128], P('space'), may hold values from -6 to 6
- blocks: bfloat16 [5, 384, 128, 128], P(None, 'space'), may hold values from -0.25 to 0.25
- precond: bfloat16 [384, 128, 128], P('space'), may hold values from -0.5 to 0.5
- couple: int32 [384, 5], P('space'), may hold values from -2 to 2
Outputs:
- corrected: float32 [1024, 384, 128], P('tm', 'space')
The draws below stay inside these ranges and needn't reach their ends.
Inputs may be any that keep to these rules, and one draw needn't show every extreme that they name: Row j, slot s couples to block row j + couple[j, s].
All inputs are finite; a program needn't handle non-finite values.
Results may differ from the reference program's by a relative error of at most 0.002.
Values may be sent and summed in bfloat16 or wider, within the bound.
No kernel may reach another device: no remote copies, remote signals or barrier semaphores. Data moves between devices by JAX's collectives and lax.ppermute only.
A program may use at most 64 MiB of HBM per device.

```python
import math
import jax
import jax.numpy as jnp

BS = 128
SWEEPS = 2
NT = 1024
NB = 384


def touch_ends(drawn, own_key, smallest, high):
    dims = drawn.shape
    place = [jax.random.randint(jax.random.fold_in(own_key, axis), (), 0, dims[axis]) for axis in range(len(dims))]
    drawn = drawn.at[tuple(place)].set(smallest)
    longest = dims.index(max(dims))
    place[longest] = (place[longest] + 1) % dims[longest]
    return drawn.at[tuple(place)].set(high)


def block_scale(own_key, shape, pieces, smallest, high):
    def one(axis_at, shards_of):
        draws = jax.random.uniform(jax.random.fold_in(jax.random.fold_in(own_key, 6), axis_at), (shards_of,), jnp.float32, smallest / len(pieces), high / len(pieces))
        return jnp.repeat(jnp.exp(draws), shape[axis_at] // shards_of).reshape((-1,) + (1,) * (len(shape) - axis_at - 1))

    factor_of = one(*pieces[0])
    for cut in pieces[1:]:
        factor_of = factor_of * one(*cut)
    return factor_of


def noise(stream_key, shape, scale, bound, pieces=(), kind=jnp.bfloat16):
    drawn = jax.random.normal(stream_key, shape, jnp.float32) * scale
    if len(pieces) > 0:
        drawn = block_scale(stream_key, shape, pieces, -0.22, 0.18) * drawn
    return jnp.clip(drawn, min=-bound, max=bound).astype(kind)


def setup_inputs(seed: int = 0) -> dict:
    splits = jax.random.split(jax.random.key(seed), 7)
    return {
        "state": noise(splits[0], (NT, NB, BS), 1.0, 6.0, ((0, 32), (1, 16)), jnp.float32),
        "forcing": noise(splits[1], (NT, NB, BS), 1.0, 6.0, ((0, 32), (1, 16)), jnp.float32),
        "initial": noise(splits[2], (NB, BS), 1.0, 6.0, ((0, 16),), jnp.float32),
        "blocks": noise(splits[3], (5, NB, BS, BS), (5 * BS) ** -0.5, 0.25, ((1, 16),)),
        "precond": noise(splits[4], (NB, BS, BS), BS ** -0.5, 0.5, ((0, 16),)),
        "couple": touch_ends(jax.random.randint(splits[5], (NB, 5), -2, 3), jax.random.fold_in(splits[5], 1), -2, 2).astype(jnp.int32),
    }


alpha_rate = 0.5
time_step = 0.5
relaxation = 0.7


def neighbour_rows(padded, couple, column, width):
    chosen = padded[:, 2:2 + width]
    for offset in range(-2, 3):
        picked = (couple[:, column] == offset)[None, :, None]
        chosen = jnp.where(picked, padded[:, 2 + offset:2 + offset + width], chosen)
    return chosen


def apply_blocks(vectors, blocks, couple):
    rounded = vectors.astype(jnp.bfloat16)
    width = rounded.shape[1]
    padded = jnp.pad(rounded, ((0, 0), (2, 2), (0, 0)))
    total = jnp.zeros(vectors.shape, jnp.float32)
    for column in range(5):
        chosen = neighbour_rows(padded, couple, column, width)
        total = total + jnp.einsum('fbj,bij->fbi', chosen.astype(jnp.float32), blocks[column].astype(jnp.float32))
    return total


def precondition(vectors, precond):
    rounded = vectors.astype(jnp.bfloat16).astype(jnp.float32)
    return jnp.einsum('fbj,bij->fbi', rounded, precond.astype(jnp.float32))


def reference(state, forcing, initial, blocks, precond, couple):
    total_steps = state.shape[0]
    previous = jnp.concatenate([initial[None], state[:-1]], 0)
    squares = (0.5 * state * state).astype(jnp.bfloat16)
    flux = apply_blocks(squares.astype(jnp.float32), blocks, couple)
    residual = forcing - state + previous - time_step * flux
    steps_index = jnp.arange(total_steps).astype(jnp.float32)
    log_rate = math.log(alpha_rate) / total_steps
    scaled = residual * jnp.exp(steps_index * log_rate)[:, None, None]
    spectrum = jnp.fft.fft(scaled, axis=0)
    spec_re = jnp.real(spectrum).astype(jnp.float32)
    spec_im = jnp.imag(spectrum).astype(jnp.float32)
    theta = 2.0 * math.pi * steps_index / total_steps
    rate = math.exp(log_rate)
    lam_re = (1.0 - rate * jnp.cos(theta))[:, None, None]
    lam_im = (rate * jnp.sin(theta))[:, None, None]
    denom = (1.0 + lam_re) ** 2 + lam_im ** 2
    coef_re = (1.0 + lam_re) / denom
    coef_im = -lam_im / denom
    sol_re = jnp.zeros(state.shape, jnp.float32)
    sol_im = jnp.zeros(state.shape, jnp.float32)
    for sweep in range(SWEEPS):
        applied = apply_blocks(jnp.concatenate([sol_re, sol_im], 0), blocks, couple)
        res_re = spec_re - (lam_re * sol_re - lam_im * sol_im) - time_step * applied[:total_steps]
        res_im = spec_im - (lam_re * sol_im + lam_im * sol_re) - time_step * applied[total_steps:]
        gres = precondition(jnp.concatenate([res_re, res_im], 0), precond)
        g_re = gres[:total_steps]
        g_im = gres[total_steps:]
        sol_re = sol_re + relaxation * (coef_re * g_re - coef_im * g_im)
        sol_im = sol_im + relaxation * (coef_re * g_im + coef_im * g_re)
    inverse = jnp.real(jnp.fft.ifft(sol_re + 1j * sol_im, axis=0))
    change = inverse * jnp.exp(-steps_index * log_rate)[:, None, None]
    return state + change
```

```python
import math

import jax
import jax.numpy as jnp
from jax import lax
from jax.sharding import PartitionSpec as P

alpha_rate = 0.5
time_step = 0.5
relaxation = 0.7
GROUP = 8


def exchange(low_edge, high_edge, axis):
    count = lax.axis_size(axis)
    odd = (lax.axis_index(axis) & 1) == 1
    first, second = [], []
    for i in range(count - 1):
        (first if i & 1 else second).extend([(i, i + 1), (i + 1, i)])
    got_first = lax.ppermute(jnp.where(odd, high_edge, low_edge), axis, first)
    got_second = lax.ppermute(jnp.where(odd, low_edge, high_edge), axis, second)
    low = jnp.where(odd, got_second, got_first)
    high = jnp.where(odd, got_first, got_second)
    return low, high


def extended(block):
    low, high = exchange(block[:, :2], block[:, -2:], "space")
    return jnp.concatenate([low, block, high], axis=1)


def apply_padded(padded, blocks, couple):
    width = padded.shape[1] - 4
    total = None
    for column in range(5):
        chosen = padded[:, 2 : 2 + width]
        for offset in range(-2, 3):
            picked = (couple[:, column] == offset)[None, :, None]
            chosen = jnp.where(picked, padded[:, 2 + offset : 2 + offset + width], chosen)
        term = jnp.einsum(
            "fbj,bij->fbi", chosen, blocks[column], preferred_element_type=jnp.float32
        )
        total = term if total is None else total + term
    return total


def split(value):
    high = lax.reduce_precision(value, 8, 7)
    return high.astype(jnp.bfloat16), (value - high).astype(jnp.bfloat16)


def step_matrix(power, steps):
    scale = jnp.exp2(-float(steps) * power)
    return scale, scale * (0.5 * steps) * power


def carried(power, steps, value):
    scale, couple = step_matrix(power, steps)
    return jnp.stack([scale * value[0] + couple * value[1], scale * value[1]])


def ring_carry(ends, steps):
    count = lax.axis_size("tm")
    position = lax.axis_index("tm")
    groups = count // GROUP
    inner = [[g * GROUP + i for i in range(GROUP)] for g in range(groups)]
    outer = [[g * GROUP + i for g in range(groups)] for i in range(GROUP)]
    mine = position % GROUP
    group = position // GROUP
    sent = jnp.broadcast_to(ends.astype(jnp.bfloat16)[None], (GROUP,) + ends.shape)
    got = lax.all_to_all(sent, "tm", 0, 0, axis_index_groups=inner, tiled=True)
    got = got.astype(jnp.float32)
    total = jnp.zeros_like(ends)
    before = jnp.zeros_like(ends)
    for i in range(GROUP):
        total = total + carried(jnp.float32(GROUP - 1 - i), steps, got[i])
        power = (mine - 1 - i).astype(jnp.float32)
        part = carried(jnp.maximum(power, 0.0), steps, got[i])
        before = before + jnp.where(power >= 0, part, 0.0)
    sent = jnp.broadcast_to(total.astype(jnp.bfloat16)[None], (groups,) + ends.shape)
    got = lax.all_to_all(sent, "tm", 0, 0, axis_index_groups=outer, tiled=True)
    got = got.astype(jnp.float32)
    into = jnp.zeros_like(ends)
    for g in range(groups):
        distance = (group - 1 - g) % groups
        wrapped = jnp.where(g >= group, alpha_rate, 1.0)
        part = carried((GROUP * distance).astype(jnp.float32), steps, got[g])
        into = into + wrapped * part
    closing = 1.0 / (1.0 - alpha_rate * 2.0 ** (-steps * count))
    return before + carried(mine.astype(jnp.float32), steps, closing * into)


def on_device(state, forcing, initial, blocks, precond, couple):
    steps = state.shape[0]
    position = lax.axis_index("tm")
    count = lax.axis_size("tm")
    squares = (0.5 * state * state).astype(jnp.bfloat16)
    flux = apply_padded(extended(squares), blocks, couple)
    first = jnp.where(position == 0, initial, 0.0)[None]
    residual = forcing - state + jnp.concatenate([first, state[:-1]], 0) - time_step * flux
    onward = jnp.where(position == count - 1, 0.0, state[-1:])
    rows = jnp.concatenate([residual, onward], 0)
    smooth = jnp.einsum(
        "fbj,bij->fbi", rows.astype(jnp.bfloat16), precond, preferred_element_type=jnp.float32
    )
    outer = 2.0 * rows - relaxation * smooth
    coupled = apply_padded(extended(smooth.astype(jnp.bfloat16)), blocks, couple)
    inner = relaxation * (smooth - time_step * coupled)
    pieces = jnp.concatenate(split(outer) + split(inner), 0)
    solved = jnp.einsum("fbj,bij->fbi", pieces, precond, preferred_element_type=jnp.float32)
    solved = solved.reshape((2, 2) + rows.shape).sum(1)
    lag = jnp.arange(steps)[:, None] - jnp.arange(steps)[None, :]
    once = jnp.where(lag >= 0, jnp.exp2(-(lag + 1.0)), 0.0)
    highest = lax.Precision.HIGHEST
    z = jnp.einsum("nm,mbc->nbc", once, solved[1, :steps], precision=highest)
    y = jnp.einsum("nm,mbc->nbc", once, solved[0, :steps] + z, precision=highest)
    ends = jnp.stack([y[-1] + solved[0, steps], z[-1] + solved[1, steps]])
    carry = ring_carry(ends, steps)
    index = jnp.arange(1, steps + 1, dtype=jnp.float32)[:, None, None]
    y = y + jnp.exp2(-index) * (carry[0] + 0.5 * index * carry[1])
    return state + relaxation * y


def solution(mesh):
    placed = (
        P("tm", "space", None),
        P("tm", "space", None),
        P("space", None),
        P(None, "space", None, None),
        P("space", None, None),
        P("space", None),
    )
    return jax.shard_map(
        on_device, mesh=mesh, in_specs=placed, out_specs=P("tm", "space", None), check_vma=False
    )
```

```python
import jax
import jax.numpy as jnp
from jax import lax
from jax.experimental import pallas as pl
from jax.experimental.pallas import tpu as pltpu
from jax.sharding import PartitionSpec as P

alpha_rate = 0.5
time_step = 0.5
relaxation = 0.7
GROUP = 16
EXTRA = 16
SLOTS = 5
VMEM_LIMIT = 16 * 1024 * 1024


def times_transposed(x, w):
    return lax.dot_general(x, w, (((1,), (1,)), ((), ())), preferred_element_type=jnp.float32)


def exchange(first_edge, second_edge, axis):
    count = lax.axis_size(axis)
    first, second = [], []
    for i in range(count - 1):
        (first if i & 1 else second).extend([(i, i + 1), (i + 1, i)])
    return lax.ppermute(first_edge, axis, first), lax.ppermute(second_edge, axis, second)


def is_odd():
    return (lax.axis_index("space") & 1) == 1


def fill_windows(windows, first_ref, second_ref, inside, width):
    for k in range(4):
        windows[0, 2 + k] = inside(k)
        windows[1, k] = inside(width - 4 + k)

    @pl.when(is_odd())
    def _():
        windows[0, 0:2] = second_ref[...]
        windows[1, 4:6] = first_ref[...]

    @pl.when(jnp.logical_not(is_odd()))
    def _():
        windows[0, 0:2] = first_ref[...]
        windows[1, 4:6] = second_ref[...]


def squared(state_ref, j, width, steps):
    s = state_ref[pl.ds(j, steps, stride=width), :]
    return (0.5 * s * s).astype(jnp.bfloat16)


def block_residual(j, flux, state_ref, forcing_ref, initial_ref):
    steps, lanes = flux.shape
    width = initial_ref.shape[0]
    position = lax.axis_index("tm")
    s = state_ref[pl.ds(j, steps, stride=width), :]
    f = forcing_ref[pl.ds(j, steps, stride=width), :]
    first = jnp.where(position == 0, initial_ref[pl.ds(j, 1), :], 0.0)
    row = lax.broadcasted_iota(jnp.int32, (steps, lanes), 0)
    previous = jnp.where(row == 0, jnp.broadcast_to(first, s.shape), pltpu.roll(s, 1, 0))
    residual = f - s + previous - time_step * flux
    onward = state_ref[pl.ds((steps - 1) * width + j, 1), :]
    onward = jnp.where(position == lax.axis_size("tm") - 1, 0.0, onward)
    row = lax.broadcasted_iota(jnp.int32, (EXTRA, lanes), 0)
    tail = jnp.where(row == 0, jnp.broadcast_to(onward, (EXTRA, lanes)), 0.0)
    return jnp.concatenate([residual, tail], 0)


def coupled_sum(j, at, picked, couple, blocks_ref):
    total = None
    for s in range(SLOTS):
        term = times_transposed(picked[at + couple[s, j]], blocks_ref[s, j])
        total = term if total is None else total + term
    return total


def solve_source(j, flux, state_ref, forcing_ref, initial_ref, precond_ref):
    rows = block_residual(j, flux, state_ref, forcing_ref, initial_ref)
    smooth = times_transposed(rows.astype(jnp.bfloat16), precond_ref[j])
    return 2.0 * rows - relaxation * smooth, smooth


def source_inside(couple, state_ref, forcing_ref, initial_ref, blocks_ref, precond_ref, outer_ref, smooth_ref, squares):
    width, steps, _ = squares.shape
    for j in range(width):
        squares[j] = squared(state_ref, j, width, steps)
    for j in range(2, width - 2):
        flux = coupled_sum(j, j, squares, couple, blocks_ref)
        outer, smooth = solve_source(j, flux, state_ref, forcing_ref, initial_ref, precond_ref)
        outer_ref[j - 2] = outer
        smooth_ref[j - 2] = smooth


def source_edges(couple, first_ref, second_ref, state_ref, forcing_ref, initial_ref, blocks_ref, precond_ref, outer_ref, smooth_ref, send_first, send_second, windows):
    width = initial_ref.shape[0]
    steps = windows.shape[2]
    fill_windows(windows, first_ref, second_ref, lambda k: squared(state_ref, k, width, steps), width)
    for e in range(4):
        j = e if e < 2 else width - 4 + e
        flux = coupled_sum(j, 2 + e % 2, windows.at[e // 2], couple, blocks_ref)
        outer, smooth = solve_source(j, flux, state_ref, forcing_ref, initial_ref, precond_ref)
        outer_ref[e] = outer
        smooth_ref[e] = smooth

    @pl.when(is_odd())
    def _():
        send_first[...] = smooth_ref[2:4].astype(jnp.bfloat16)
        send_second[...] = smooth_ref[0:2].astype(jnp.bfloat16)

    @pl.when(jnp.logical_not(is_odd()))
    def _():
        send_first[...] = smooth_ref[0:2].astype(jnp.bfloat16)
        send_second[...] = smooth_ref[2:4].astype(jnp.bfloat16)


def solve_block(j, coupled, outer, smooth, precond_ref, out_outer, out_inner, out_next, width):
    rows = coupled.shape[0]
    steps = rows - EXTRA
    inner = relaxation * (smooth - time_step * coupled)
    outer_high = outer.astype(jnp.bfloat16)
    outer_low = (outer - outer_high.astype(jnp.float32)).astype(jnp.bfloat16)
    inner_high = inner.astype(jnp.bfloat16)
    inner_low = (inner - inner_high.astype(jnp.float32)).astype(jnp.bfloat16)
    pieces = jnp.concatenate([outer_high, outer_low, inner_high, inner_low], 0)
    solved = times_transposed(pieces, precond_ref[j])
    outer = solved[:rows] + solved[rows : 2 * rows]
    inner = solved[2 * rows : 3 * rows] + solved[3 * rows :]
    out_outer[pl.ds(j, steps, stride=width), :] = outer[:steps]
    out_inner[pl.ds(j, steps, stride=width), :] = inner[:steps]
    out_next[pl.ds(j, 1), :] = outer[steps : steps + 1]
    out_next[pl.ds(width + j, 1), :] = inner[steps : steps + 1]


def solve_inside(couple, all_inside_ref, all_edges_ref, outer_ref, blocks_ref, precond_ref, out_outer, out_inner, out_next, rounded):
    width = rounded.shape[0]
    for k in range(2):
        rounded[k] = all_edges_ref[k].astype(jnp.bfloat16)
        rounded[width - 2 + k] = all_edges_ref[2 + k].astype(jnp.bfloat16)
    for k in range(width - 4):
        rounded[2 + k] = all_inside_ref[k].astype(jnp.bfloat16)
    out_outer[...] = jnp.zeros_like(out_outer)
    out_inner[...] = jnp.zeros_like(out_inner)
    out_next[...] = jnp.zeros_like(out_next)
    for j in range(2, width - 2):
        coupled = coupled_sum(j, j, rounded, couple, blocks_ref)
        solve_block(j, coupled, outer_ref[j - 2], all_inside_ref[j - 2], precond_ref, out_outer, out_inner, out_next, width)


def solve_edges(couple, first_ref, second_ref, all_inside_ref, all_edges_ref, outer_ref, blocks_ref, precond_ref, in_outer, in_inner, in_next, state_ref, result_ref, ends_ref, windows, my_outer, my_inner, my_next):
    width = in_next.shape[0] // 2
    steps = in_outer.shape[0] // width

    def inside(k):
        if k < 2:
            return all_edges_ref[k].astype(jnp.bfloat16)
        if k >= width - 2:
            return all_edges_ref[k - width + 4].astype(jnp.bfloat16)
        return all_inside_ref[k - 2].astype(jnp.bfloat16)

    fill_windows(windows, first_ref, second_ref, inside, width)
    my_outer[...] = in_outer[...]
    my_inner[...] = in_inner[...]
    my_next[...] = in_next[...]
    for e in range(4):
        j = e if e < 2 else width - 4 + e
        coupled = coupled_sum(j, 2 + e % 2, windows.at[e // 2], couple, blocks_ref)
        solve_block(j, coupled, outer_ref[e], all_edges_ref[e], precond_ref, my_outer, my_inner, my_next, width)
    z = jnp.zeros((width, 128), jnp.float32)
    y = jnp.zeros((width, 128), jnp.float32)
    for n in range(steps):
        rows = pl.ds(n * width, width)
        z = 0.5 * (my_inner[rows, :] + z)
        y = 0.5 * (my_outer[rows, :] + z + y)
        result_ref[rows, :] = state_ref[rows, :] + relaxation * y
    ends_outer = (y + my_next[pl.ds(0, width), :]).astype(jnp.bfloat16)
    ends_inner = (z + my_next[pl.ds(width, width), :]).astype(jnp.bfloat16)
    for k in range(ends_ref.shape[0]):
        ends_ref[k, 0] = ends_outer
        ends_ref[k, 1] = ends_inner


def finish_kernel(local_ref, carry_ref, out_ref):
    width = carry_ref.shape[1]
    steps = out_ref.shape[0] // width
    for n in range(steps):
        rows = pl.ds(n * width, width)
        scale = relaxation * 0.5 ** (n + 1)
        out_ref[rows, :] = local_ref[rows, :] + scale * (carry_ref[0] + (0.5 * (n + 1)) * carry_ref[1])


def carried(power, steps, value):
    scale = jnp.exp2(-float(steps) * power)
    return jnp.stack([scale * value[0] + scale * (0.5 * steps) * power * value[1], scale * value[1]])


def ring_carry(sent, steps):
    count = lax.axis_size("tm")
    position = lax.axis_index("tm")
    groups = count // GROUP
    members = [[g * GROUP + i for i in range(GROUP)] for g in range(groups)]
    mine = position % GROUP
    group = position // GROUP
    got = lax.all_to_all(sent, "tm", 0, 0, axis_index_groups=members, tiled=True)
    got = got.astype(jnp.float32)
    total = jnp.zeros(got.shape[1:], jnp.float32)
    before = total
    for i in range(GROUP):
        total = total + carried(jnp.float32(GROUP - 1 - i), steps, got[i])
        power = (mine - 1 - i).astype(jnp.float32)
        part = carried(jnp.maximum(power, 0.0), steps, got[i])
        before = before + jnp.where(power >= 0, part, 0.0)
    total = total.astype(jnp.bfloat16)
    into = jnp.zeros(got.shape[1:], jnp.float32)
    for m in range(1, groups + 1):
        other = total
        if m < groups:
            route = [(i, (i + m * GROUP) % count) for i in range(count)]
            other = lax.ppermute(total, "tm", route)
        wrapped = jnp.where(m > group, alpha_rate, 1.0)
        power = jnp.float32(GROUP * (m - 1))
        into = into + wrapped * carried(power, steps, other.astype(jnp.float32))
    closing = 1.0 / (1.0 - alpha_rate * 2.0 ** (-steps * count))
    return before + carried(mine.astype(jnp.float32), steps, closing * into)


def on_device(state, forcing, initial, blocks, precond, couple):
    steps, width, lanes = state.shape
    rows = steps + EXTRA
    flat = (steps * width, lanes)
    state2 = state.reshape(flat)
    forcing2 = forcing.reshape(flat)
    couple = couple.T
    f32, bf16 = jnp.float32, jnp.bfloat16

    def shaped(shape, kind=f32):
        return jax.ShapeDtypeStruct(shape, kind)

    def run(kernel, operands, results, scratch, block_rows, passes, scalars=1):
        scalar = [pl.BlockSpec(memory_space=pltpu.SMEM)] * scalars
        vector = pl.BlockSpec(memory_space=pltpu.VMEM)
        return pl.pallas_call(
            kernel,
            out_shape=results,
            in_specs=scalar + [vector] * (len(operands) - scalars),
            out_specs=[vector] * len(results),
            scratch_shapes=scratch,
            compiler_params=pltpu.CompilerParams(vmem_limit_bytes=VMEM_LIMIT),
            cost_estimate=pl.CostEstimate(
                flops=block_rows * passes * 2 * rows * lanes * lanes,
                bytes_accessed=block_rows * 6 * lanes * lanes * 2 + 1000000,
                transcendentals=0,
            ),
            name=kernel.__name__,
        )(*operands)

    low_edge = (0.5 * state[:, :2] * state[:, :2]).astype(bf16).transpose(1, 0, 2)
    high_edge = (0.5 * state[:, -2:] * state[:, -2:]).astype(bf16).transpose(1, 0, 2)
    odd = is_odd()
    first, second = exchange(
        jnp.where(odd, high_edge, low_edge), jnp.where(odd, low_edge, high_edge), "space"
    )

    outer_in, smooth_in = run(
        source_inside,
        (couple, state2, forcing2, initial, blocks, precond),
        [shaped((width - 4, rows, lanes))] * 2,
        [pltpu.VMEM((width, steps, lanes), bf16)],
        width - 4,
        6,
    )
    outer_ed, smooth_ed, send_first, send_second = run(
        source_edges,
        (couple, first, second, state2, forcing2, initial, blocks, precond),
        [shaped((4, rows, lanes))] * 2 + [shaped((2, rows, lanes), bf16)] * 2,
        [pltpu.VMEM((2, 6, steps, lanes), bf16)],
        4,
        6,
    )
    first, second = exchange(send_first, send_second, "space")
    out_outer, out_inner, out_next = run(
        solve_inside,
        (couple, smooth_in, smooth_ed, outer_in, blocks, precond),
        [shaped(flat), shaped(flat), shaped((2 * width, lanes))],
        [pltpu.VMEM((width, rows, lanes), bf16)],
        width - 4,
        9,
    )
    local, ends = run(
        solve_edges,
        (couple, first, second, smooth_in, smooth_ed, outer_ed, blocks, precond, out_outer, out_inner, out_next, state2),
        [shaped(flat), shaped((GROUP, 2, width, lanes), bf16)],
        [
            pltpu.VMEM((2, 6, rows, lanes), bf16),
            pltpu.VMEM(flat, f32),
            pltpu.VMEM(flat, f32),
            pltpu.VMEM((2 * width, lanes), f32),
        ],
        4,
        9,
    )
    carry = ring_carry(ends, steps)
    (out,) = run(finish_kernel, (local, carry), [shaped(flat)], [], 1, 1, 0)
    return out.reshape(state.shape)


def solution(mesh):
    placed = (
        P("tm", "space", None),
        P("tm", "space", None),
        P("space", None),
        P(None, "space", None, None),
        P("space", None, None),
        P("space", None),
    )
    return jax.shard_map(
        on_device, mesh=mesh, in_specs=placed, out_specs=P("tm", "space", None), check_vma=False
    )
```

```python
import jax
import jax.numpy as jnp
from jax import lax
from jax.experimental import pallas as pl
from jax.experimental.pallas import tpu as pltpu
from jax.sharding import PartitionSpec as P

alpha_rate = 0.5
time_step = 0.5
relaxation = 0.7
GROUP = 16
EXTRA = 16
SLOTS = 5
PREFETCH_ROWS = 400
VMEM_LIMIT = 16 * 1024 * 1024


def times_transposed(x, w):
    return lax.dot_general(x, w, (((1,), (1,)), ((), ())), preferred_element_type=jnp.float32)


def exchange(first_edge, second_edge, axis):
    count = lax.axis_size(axis)
    first, second = [], []
    for i in range(count - 1):
        (first if i & 1 else second).extend([(i, i + 1), (i + 1, i)])
    return lax.ppermute(first_edge, axis, first), lax.ppermute(second_edge, axis, second)


def is_odd():
    return (lax.axis_index("space") & 1) == 1


def fill_windows(windows, first_ref, second_ref, inside, width):
    for k in range(4):
        windows[0, 2 + k] = inside(k)
        windows[1, k] = inside(width - 4 + k)

    @pl.when(is_odd())
    def _():
        windows[0, 0:2] = second_ref[...]
        windows[1, 4:6] = first_ref[...]

    @pl.when(jnp.logical_not(is_odd()))
    def _():
        windows[0, 0:2] = first_ref[...]
        windows[1, 4:6] = second_ref[...]


def squared(state_ref, j, width, steps):
    s = state_ref[pl.ds(j, steps, stride=width), :]
    return (0.5 * s * s).astype(jnp.bfloat16)


def block_residual(j, flux, state_ref, forcing_ref, initial_ref):
    steps, lanes = flux.shape
    width = initial_ref.shape[0]
    position = lax.axis_index("tm")
    s = state_ref[pl.ds(j, steps, stride=width), :]
    f = forcing_ref[pl.ds(j, steps, stride=width), :]
    first = jnp.where(position == 0, initial_ref[pl.ds(j, 1), :], 0.0)
    row = lax.broadcasted_iota(jnp.int32, (steps, lanes), 0)
    previous = jnp.where(row == 0, jnp.broadcast_to(first, s.shape), pltpu.roll(s, 1, 0))
    residual = f - s + previous - time_step * flux
    onward = state_ref[pl.ds((steps - 1) * width + j, 1), :]
    onward = jnp.where(position == lax.axis_size("tm") - 1, 0.0, onward)
    row = lax.broadcasted_iota(jnp.int32, (EXTRA, lanes), 0)
    tail = jnp.where(row == 0, jnp.broadcast_to(onward, (EXTRA, lanes)), 0.0)
    return jnp.concatenate([residual, tail], 0)


def coupled_sum(j, at, picked, couple, blocks_ref):
    rows = jnp.concatenate([picked[at + couple[s, j]] for s in range(SLOTS)], 1)
    weights = jnp.concatenate([blocks_ref[s, j] for s in range(SLOTS)], 1)
    return times_transposed(rows, weights)


def solve_source(j, flux, state_ref, forcing_ref, initial_ref, precond_ref):
    rows = block_residual(j, flux, state_ref, forcing_ref, initial_ref)
    smooth = times_transposed(rows.astype(jnp.bfloat16), precond_ref[j])
    return 2.0 * rows - relaxation * smooth, smooth


def edge_squares(state_ref, send_first, send_second):
    _, steps, _ = send_first.shape
    width = state_ref.shape[0] // steps

    @pl.when(is_odd())
    def _():
        for k in range(2):
            send_first[k] = squared(state_ref, width - 2 + k, width, steps)
            send_second[k] = squared(state_ref, k, width, steps)

    @pl.when(jnp.logical_not(is_odd()))
    def _():
        for k in range(2):
            send_first[k] = squared(state_ref, k, width, steps)
            send_second[k] = squared(state_ref, width - 2 + k, width, steps)


def source_inside(couple, state_ref, forcing_ref, initial_ref, blocks_ref, precond_ref, outer_ref, smooth_ref, squares):
    width, steps, _ = squares.shape
    for j in range(width):
        squares[j] = squared(state_ref, j, width, steps)
    for j in range(2, width - 2):
        flux = coupled_sum(j, j, squares, couple, blocks_ref)
        outer, smooth = solve_source(j, flux, state_ref, forcing_ref, initial_ref, precond_ref)
        outer_ref[j - 2] = outer
        smooth_ref[j - 2] = smooth


def source_edges(couple, first_ref, second_ref, state_ref, forcing_ref, initial_ref, blocks_ref, precond_ref, outer_ref, smooth_ref, send_first, send_second, windows):
    width = initial_ref.shape[0]
    steps = windows.shape[2]
    fill_windows(windows, first_ref, second_ref, lambda k: squared(state_ref, k, width, steps), width)
    for e in range(4):
        j = e if e < 2 else width - 4 + e
        flux = coupled_sum(j, 2 + e % 2, windows.at[e // 2], couple, blocks_ref)
        outer, smooth = solve_source(j, flux, state_ref, forcing_ref, initial_ref, precond_ref)
        outer_ref[e] = outer
        smooth_ref[e] = smooth

    @pl.when(is_odd())
    def _():
        send_first[...] = smooth_ref[2:4].astype(jnp.bfloat16)
        send_second[...] = smooth_ref[0:2].astype(jnp.bfloat16)

    @pl.when(jnp.logical_not(is_odd()))
    def _():
        send_first[...] = smooth_ref[0:2].astype(jnp.bfloat16)
        send_second[...] = smooth_ref[2:4].astype(jnp.bfloat16)


def solve_block(j, coupled, outer, smooth, precond_ref, out_outer, out_inner, out_next, width):
    rows = coupled.shape[0]
    steps = rows - EXTRA
    inner = relaxation * (smooth - time_step * coupled)
    outer_high = outer.astype(jnp.bfloat16)
    outer_low = (outer - outer_high.astype(jnp.float32)).astype(jnp.bfloat16)
    inner_high = inner.astype(jnp.bfloat16)
    inner_low = (inner - inner_high.astype(jnp.float32)).astype(jnp.bfloat16)
    pieces = jnp.concatenate([outer_high, outer_low, inner_high, inner_low], 0)
    solved = times_transposed(pieces, precond_ref[j])
    outer = solved[:rows] + solved[rows : 2 * rows]
    inner = solved[2 * rows : 3 * rows] + solved[3 * rows :]
    out_outer[pl.ds(j, steps, stride=width), :] = outer[:steps]
    out_inner[pl.ds(j, steps, stride=width), :] = inner[:steps]
    out_next[pl.ds(j, 1), :] = outer[steps : steps + 1]
    out_next[pl.ds(width + j, 1), :] = inner[steps : steps + 1]


def solve_inside(couple, all_inside_ref, all_edges_ref, outer_ref, blocks_ref, precond_ref, out_outer, out_inner, out_next, rounded):
    width = rounded.shape[0]
    for k in range(2):
        rounded[k] = all_edges_ref[k].astype(jnp.bfloat16)
        rounded[width - 2 + k] = all_edges_ref[2 + k].astype(jnp.bfloat16)
    for k in range(width - 4):
        rounded[2 + k] = all_inside_ref[k].astype(jnp.bfloat16)
    out_outer[...] = jnp.zeros_like(out_outer)
    out_inner[...] = jnp.zeros_like(out_inner)
    out_next[...] = jnp.zeros_like(out_next)
    for j in range(2, width - 2):
        coupled = coupled_sum(j, j, rounded, couple, blocks_ref)
        solve_block(j, coupled, outer_ref[j - 2], all_inside_ref[j - 2], precond_ref, out_outer, out_inner, out_next, width)


def solve_edges(couple, first_ref, second_ref, all_inside_ref, all_edges_ref, outer_ref, blocks_ref, precond_ref, in_outer, in_inner, in_next, state_ref, result_ref, ends_ref, windows, my_outer, my_inner, my_next):
    width = in_next.shape[0] // 2
    steps = in_outer.shape[0] // width

    def inside(k):
        if k < 2:
            return all_edges_ref[k].astype(jnp.bfloat16)
        if k >= width - 2:
            return all_edges_ref[k - width + 4].astype(jnp.bfloat16)
        return all_inside_ref[k - 2].astype(jnp.bfloat16)

    fill_windows(windows, first_ref, second_ref, inside, width)
    my_outer[...] = in_outer[...]
    my_inner[...] = in_inner[...]
    my_next[...] = in_next[...]
    for e in range(4):
        j = e if e < 2 else width - 4 + e
        coupled = coupled_sum(j, 2 + e % 2, windows.at[e // 2], couple, blocks_ref)
        solve_block(j, coupled, outer_ref[e], all_edges_ref[e], precond_ref, my_outer, my_inner, my_next, width)
    z = jnp.zeros((width, 128), jnp.float32)
    y = jnp.zeros((width, 128), jnp.float32)
    for n in range(steps):
        rows = pl.ds(n * width, width)
        z = 0.5 * (my_inner[rows, :] + z)
        y = 0.5 * (my_outer[rows, :] + z + y)
        result_ref[rows, :] = state_ref[rows, :] + relaxation * y
    ends_outer = (y + my_next[pl.ds(0, width), :]).astype(jnp.bfloat16)
    ends_inner = (z + my_next[pl.ds(width, width), :]).astype(jnp.bfloat16)
    for k in range(ends_ref.shape[0]):
        ends_ref[k, 0] = ends_outer
        ends_ref[k, 1] = ends_inner


def finish_kernel(local_ref, carry_ref, out_ref):
    width = carry_ref.shape[1]
    steps = out_ref.shape[0] // width
    for n in range(steps):
        rows = pl.ds(n * width, width)
        scale = relaxation * 0.5 ** (n + 1)
        out_ref[rows, :] = local_ref[rows, :] + scale * (carry_ref[0] + (0.5 * (n + 1)) * carry_ref[1])


def carried(power, steps, value):
    scale = jnp.exp2(-float(steps) * power)
    return jnp.stack([scale * value[0] + scale * (0.5 * steps) * power * value[1], scale * value[1]])


def ring_carry(sent, steps):
    count = lax.axis_size("tm")
    position = lax.axis_index("tm")
    groups = count // GROUP
    members = [[g * GROUP + i for i in range(GROUP)] for g in range(groups)]
    mine = position % GROUP
    group = position // GROUP
    got = lax.all_to_all(sent, "tm", 0, 0, axis_index_groups=members, tiled=True)
    got = got.astype(jnp.float32)
    total = jnp.zeros(got.shape[1:], jnp.float32)
    before = total
    for i in range(GROUP):
        total = total + carried(jnp.float32(GROUP - 1 - i), steps, got[i])
        power = (mine - 1 - i).astype(jnp.float32)
        part = carried(jnp.maximum(power, 0.0), steps, got[i])
        before = before + jnp.where(power >= 0, part, 0.0)
    total = total.astype(jnp.bfloat16)
    into = jnp.zeros(got.shape[1:], jnp.float32)
    for m in range(1, groups + 1):
        other = total
        if m < groups:
            route = [(i, (i + m * GROUP) % count) for i in range(count)]
            other = lax.ppermute(total, "tm", route)
        wrapped = jnp.where(m > group, alpha_rate, 1.0)
        power = jnp.float32(GROUP * (m - 1))
        into = into + wrapped * carried(power, steps, other.astype(jnp.float32))
    closing = 1.0 / (1.0 - alpha_rate * 2.0 ** (-steps * count))
    return before + carried(mine.astype(jnp.float32), steps, closing * into)


def on_device(state, forcing, initial, blocks, precond, couple):
    steps, width, lanes = state.shape
    rows = steps + EXTRA
    flat = (steps * width, lanes)
    state2 = state.reshape(flat)
    forcing2 = forcing.reshape(flat)
    couple = couple.T
    f32, bf16 = jnp.float32, jnp.bfloat16

    def shaped(shape, kind=f32):
        return jax.ShapeDtypeStruct(shape, kind)

    def run(kernel, operands, results, scratch, block_rows, passes, scalars=1):
        scalar = [pl.BlockSpec(memory_space=pltpu.SMEM)] * scalars
        vector = pl.BlockSpec(memory_space=pltpu.VMEM)
        return pl.pallas_call(
            kernel,
            out_shape=results,
            in_specs=scalar + [vector] * (len(operands) - scalars),
            out_specs=[vector] * len(results),
            scratch_shapes=scratch,
            compiler_params=pltpu.CompilerParams(vmem_limit_bytes=VMEM_LIMIT),
            cost_estimate=pl.CostEstimate(
                flops=block_rows * passes * 2 * rows * lanes * lanes,
                bytes_accessed=block_rows * 6 * lanes * lanes * 2 + 1000000,
                transcendentals=0,
            ),
            name=kernel.__name__,
        )(*operands)

    send_first, send_second = run(
        edge_squares, (state2,), [shaped((2, steps, lanes), bf16)] * 2, [], PREFETCH_ROWS, 6, 0
    )
    first, second = exchange(send_first, send_second, "space")

    outer_in, smooth_in = run(
        source_inside,
        (couple, state2, forcing2, initial, blocks, precond),
        [shaped((width - 4, rows, lanes))] * 2,
        [pltpu.VMEM((width, steps, lanes), bf16)],
        width - 4,
        6,
    )
    outer_ed, smooth_ed, send_first, send_second = run(
        source_edges,
        (couple, first, second, state2, forcing2, initial, blocks, precond),
        [shaped((4, rows, lanes))] * 2 + [shaped((2, rows, lanes), bf16)] * 2,
        [pltpu.VMEM((2, 6, steps, lanes), bf16)],
        4,
        6,
    )
    first, second = exchange(send_first, send_second, "space")
    out_outer, out_inner, out_next = run(
        solve_inside,
        (couple, smooth_in, smooth_ed, outer_in, blocks, precond),
        [shaped(flat), shaped(flat), shaped((2 * width, lanes))],
        [pltpu.VMEM((width, rows, lanes), bf16)],
        width - 4,
        9,
    )
    local, ends = run(
        solve_edges,
        (couple, first, second, smooth_in, smooth_ed, outer_ed, blocks, precond, out_outer, out_inner, out_next, state2),
        [shaped(flat), shaped((GROUP, 2, width, lanes), bf16)],
        [
            pltpu.VMEM((2, 6, rows, lanes), bf16),
            pltpu.VMEM(flat, f32),
            pltpu.VMEM(flat, f32),
            pltpu.VMEM((2 * width, lanes), f32),
        ],
        4,
        9,
    )
    carry = ring_carry(ends, steps)
    (out,) = run(finish_kernel, (local, carry), [shaped(flat)], [], 1, 1, 0)
    return out.reshape(state.shape)


def solution(mesh):
    placed = (
        P("tm", "space", None),
        P("tm", "space", None),
        P("space", None),
        P(None, "space", None, None),
        P("space", None, None),
        P("space", None),
    )
    return jax.shard_map(
        on_device, mesh=mesh, in_specs=placed, out_specs=P("tm", "space", None), check_vma=False
    )
```

```python
import jax
import jax.numpy as jnp
from jax import lax
from jax.experimental import pallas as pl
from jax.experimental.pallas import tpu as pltpu
from jax.sharding import PartitionSpec as P

alpha_rate = 0.5
time_step = 0.5
relaxation = 0.7
GROUP = 16
EXTRA = 16
SLOTS = 5
PREFETCH_ROWS = 400
VMEM_LIMIT = 16 * 1024 * 1024


def times_transposed(x, w):
    return lax.dot_general(x, w, (((1,), (1,)), ((), ())), preferred_element_type=jnp.float32)


def exchange(first_edge, second_edge, axis):
    count = lax.axis_size(axis)
    first, second = [], []
    for i in range(count - 1):
        (first if i & 1 else second).extend([(i, i + 1), (i + 1, i)])
    return lax.ppermute(first_edge, axis, first), lax.ppermute(second_edge, axis, second)


def is_odd():
    return (lax.axis_index("space") & 1) == 1


def fill_windows(windows, first_ref, second_ref, inside, width):
    for k in range(4):
        windows[0, 2 + k] = inside(k)
        windows[1, k] = inside(width - 4 + k)

    @pl.when(is_odd())
    def _():
        windows[0, 0:2] = second_ref[...]
        windows[1, 4:6] = first_ref[...]

    @pl.when(jnp.logical_not(is_odd()))
    def _():
        windows[0, 0:2] = first_ref[...]
        windows[1, 4:6] = second_ref[...]


def squared(state_ref, j, width, steps):
    s = state_ref[pl.ds(j, steps, stride=width), :]
    return (0.5 * s * s).astype(jnp.bfloat16)


def block_residual(j, flux, state_ref, forcing_ref, initial_ref):
    steps, lanes = flux.shape
    width = initial_ref.shape[0]
    position = lax.axis_index("tm")
    s = state_ref[pl.ds(j, steps, stride=width), :]
    f = forcing_ref[pl.ds(j, steps, stride=width), :]
    first = jnp.where(position == 0, initial_ref[pl.ds(j, 1), :], 0.0)
    row = lax.broadcasted_iota(jnp.int32, (steps, lanes), 0)
    previous = jnp.where(row == 0, jnp.broadcast_to(first, s.shape), pltpu.roll(s, 1, 0))
    residual = f - s + previous - time_step * flux
    onward = state_ref[pl.ds((steps - 1) * width + j, 1), :]
    onward = jnp.where(position == lax.axis_size("tm") - 1, 0.0, onward)
    row = lax.broadcasted_iota(jnp.int32, (EXTRA, lanes), 0)
    tail = jnp.where(row == 0, jnp.broadcast_to(onward, (EXTRA, lanes)), 0.0)
    return jnp.concatenate([residual, tail], 0)


def pair_product(x, w):
    rows = x[0].shape[0]
    zero = jnp.zeros_like(x[0])
    left = jnp.concatenate([jnp.concatenate([x[0], zero], 1), jnp.concatenate([zero, x[1]], 1)], 0)
    both = times_transposed(left, jnp.concatenate(w, 1))
    return both[:rows], both[rows:]


def coupled_pair(j, at, picked, couple, blocks_ref):
    deep = SLOTS - 1
    last = pair_product(
        [picked[at + k + couple[deep, j + k]] for k in range(2)],
        [blocks_ref[deep, j + k] for k in range(2)],
    )
    total = []
    for k in range(2):
        rows = jnp.concatenate([picked[at + k + couple[s, j + k]] for s in range(deep)], 1)
        weights = jnp.concatenate([blocks_ref[s, j + k] for s in range(deep)], 1)
        total.append(times_transposed(rows, weights) + last[k])
    return total


def solve_source(j, flux, state_ref, forcing_ref, initial_ref, precond_ref):
    rows = [block_residual(j + k, flux[k], state_ref, forcing_ref, initial_ref) for k in range(2)]
    smooth = pair_product(
        [r.astype(jnp.bfloat16) for r in rows], [precond_ref[j + k] for k in range(2)]
    )
    return [2.0 * rows[k] - relaxation * smooth[k] for k in range(2)], smooth


def edge_squares(state_ref, send_first, send_second):
    _, steps, _ = send_first.shape
    width = state_ref.shape[0] // steps

    @pl.when(is_odd())
    def _():
        for k in range(2):
            send_first[k] = squared(state_ref, width - 2 + k, width, steps)
            send_second[k] = squared(state_ref, k, width, steps)

    @pl.when(jnp.logical_not(is_odd()))
    def _():
        for k in range(2):
            send_first[k] = squared(state_ref, k, width, steps)
            send_second[k] = squared(state_ref, width - 2 + k, width, steps)


def source_inside(couple, state_ref, forcing_ref, initial_ref, blocks_ref, precond_ref, outer_ref, smooth_ref, squares):
    width, steps, _ = squares.shape
    for j in range(width):
        squares[j] = squared(state_ref, j, width, steps)
    for j in range(2, width - 2, 2):
        flux = coupled_pair(j, j, squares, couple, blocks_ref)
        outer, smooth = solve_source(j, flux, state_ref, forcing_ref, initial_ref, precond_ref)
        for k in range(2):
            outer_ref[j - 2 + k] = outer[k]
            smooth_ref[j - 2 + k] = smooth[k]


def source_edges(couple, first_ref, second_ref, state_ref, forcing_ref, initial_ref, blocks_ref, precond_ref, outer_ref, smooth_ref, send_first, send_second, windows):
    width = initial_ref.shape[0]
    steps = windows.shape[2]
    fill_windows(windows, first_ref, second_ref, lambda k: squared(state_ref, k, width, steps), width)
    for e in range(2):
        j = e * (width - 2)
        flux = coupled_pair(j, 2, windows.at[e], couple, blocks_ref)
        outer, smooth = solve_source(j, flux, state_ref, forcing_ref, initial_ref, precond_ref)
        for k in range(2):
            outer_ref[2 * e + k] = outer[k]
            smooth_ref[2 * e + k] = smooth[k]

    @pl.when(is_odd())
    def _():
        send_first[...] = smooth_ref[2:4].astype(jnp.bfloat16)
        send_second[...] = smooth_ref[0:2].astype(jnp.bfloat16)

    @pl.when(jnp.logical_not(is_odd()))
    def _():
        send_first[...] = smooth_ref[0:2].astype(jnp.bfloat16)
        send_second[...] = smooth_ref[2:4].astype(jnp.bfloat16)


def split(value):
    high = value.astype(jnp.bfloat16)
    return [high, (value - high.astype(jnp.float32)).astype(jnp.bfloat16)]


def solve_pair(j, coupled, outer, smooth, precond_ref, out_outer, out_inner, out_next, width):
    rows = coupled[0].shape[0]
    steps = rows - EXTRA
    pieces = []
    for k in range(2):
        inner = relaxation * (smooth[k] - time_step * coupled[k])
        pieces.append(jnp.concatenate(split(outer[k]) + split(inner), 0))
    solved = pair_product(pieces, [precond_ref[j + k] for k in range(2)])
    for k in range(2):
        outer_k = solved[k][:rows] + solved[k][rows : 2 * rows]
        inner_k = solved[k][2 * rows : 3 * rows] + solved[k][3 * rows :]
        out_outer[pl.ds(j + k, steps, stride=width), :] = outer_k[:steps]
        out_inner[pl.ds(j + k, steps, stride=width), :] = inner_k[:steps]
        out_next[pl.ds(j + k, 1), :] = outer_k[steps : steps + 1]
        out_next[pl.ds(width + j + k, 1), :] = inner_k[steps : steps + 1]


def solve_inside(couple, all_inside_ref, all_edges_ref, outer_ref, blocks_ref, precond_ref, out_outer, out_inner, out_next, rounded):
    width = rounded.shape[0]
    for k in range(2):
        rounded[k] = all_edges_ref[k].astype(jnp.bfloat16)
        rounded[width - 2 + k] = all_edges_ref[2 + k].astype(jnp.bfloat16)
    for k in range(width - 4):
        rounded[2 + k] = all_inside_ref[k].astype(jnp.bfloat16)
    out_outer[...] = jnp.zeros_like(out_outer)
    out_inner[...] = jnp.zeros_like(out_inner)
    out_next[...] = jnp.zeros_like(out_next)
    for j in range(2, width - 2, 2):
        coupled = coupled_pair(j, j, rounded, couple, blocks_ref)
        outer = [outer_ref[j - 2 + k] for k in range(2)]
        smooth = [all_inside_ref[j - 2 + k] for k in range(2)]
        solve_pair(j, coupled, outer, smooth, precond_ref, out_outer, out_inner, out_next, width)


def solve_edges(couple, first_ref, second_ref, all_inside_ref, all_edges_ref, outer_ref, blocks_ref, precond_ref, in_outer, in_inner, in_next, state_ref, result_ref, ends_ref, windows, my_outer, my_inner, my_next):
    width = in_next.shape[0] // 2
    steps = in_outer.shape[0] // width

    def inside(k):
        if k < 2:
            return all_edges_ref[k].astype(jnp.bfloat16)
        if k >= width - 2:
            return all_edges_ref[k - width + 4].astype(jnp.bfloat16)
        return all_inside_ref[k - 2].astype(jnp.bfloat16)

    fill_windows(windows, first_ref, second_ref, inside, width)
    my_outer[...] = in_outer[...]
    my_inner[...] = in_inner[...]
    my_next[...] = in_next[...]
    for e in range(2):
        j = e * (width - 2)
        coupled = coupled_pair(j, 2, windows.at[e], couple, blocks_ref)
        outer = [outer_ref[2 * e + k] for k in range(2)]
        smooth = [all_edges_ref[2 * e + k] for k in range(2)]
        solve_pair(j, coupled, outer, smooth, precond_ref, my_outer, my_inner, my_next, width)
    z = jnp.zeros((width, 128), jnp.float32)
    y = jnp.zeros((width, 128), jnp.float32)
    for n in range(steps):
        rows = pl.ds(n * width, width)
        z = 0.5 * (my_inner[rows, :] + z)
        y = 0.5 * (my_outer[rows, :] + z + y)
        result_ref[rows, :] = state_ref[rows, :] + relaxation * y
    ends_outer = (y + my_next[pl.ds(0, width), :]).astype(jnp.bfloat16)
    ends_inner = (z + my_next[pl.ds(width, width), :]).astype(jnp.bfloat16)
    for k in range(ends_ref.shape[0]):
        ends_ref[k, 0] = ends_outer
        ends_ref[k, 1] = ends_inner


def finish_kernel(local_ref, carry_ref, out_ref):
    width = carry_ref.shape[1]
    steps = out_ref.shape[0] // width
    for n in range(steps):
        rows = pl.ds(n * width, width)
        scale = relaxation * 0.5 ** (n + 1)
        out_ref[rows, :] = local_ref[rows, :] + scale * (carry_ref[0] + (0.5 * (n + 1)) * carry_ref[1])


def carried(power, steps, value):
    scale = jnp.exp2(-float(steps) * power)
    return jnp.stack([scale * value[0] + scale * (0.5 * steps) * power * value[1], scale * value[1]])


def ring_carry(sent, steps):
    count = lax.axis_size("tm")
    position = lax.axis_index("tm")
    groups = count // GROUP
    members = [[g * GROUP + i for i in range(GROUP)] for g in range(groups)]
    mine = position % GROUP
    group = position // GROUP
    got = lax.all_to_all(sent, "tm", 0, 0, axis_index_groups=members, tiled=True)
    got = got.astype(jnp.float32)
    total = jnp.zeros(got.shape[1:], jnp.float32)
    before = total
    for i in range(GROUP):
        total = total + carried(jnp.float32(GROUP - 1 - i), steps, got[i])
        power = (mine - 1 - i).astype(jnp.float32)
        part = carried(jnp.maximum(power, 0.0), steps, got[i])
        before = before + jnp.where(power >= 0, part, 0.0)
    total = total.astype(jnp.bfloat16)
    into = jnp.zeros(got.shape[1:], jnp.float32)
    for m in range(1, groups + 1):
        other = total
        if m < groups:
            route = [(i, (i + m * GROUP) % count) for i in range(count)]
            other = lax.ppermute(total, "tm", route)
        wrapped = jnp.where(m > group, alpha_rate, 1.0)
        power = jnp.float32(GROUP * (m - 1))
        into = into + wrapped * carried(power, steps, other.astype(jnp.float32))
    closing = 1.0 / (1.0 - alpha_rate * 2.0 ** (-steps * count))
    return before + carried(mine.astype(jnp.float32), steps, closing * into)


def on_device(state, forcing, initial, blocks, precond, couple):
    steps, width, lanes = state.shape
    rows = steps + EXTRA
    flat = (steps * width, lanes)
    state2 = state.reshape(flat)
    forcing2 = forcing.reshape(flat)
    couple = couple.T
    f32, bf16 = jnp.float32, jnp.bfloat16

    def shaped(shape, kind=f32):
        return jax.ShapeDtypeStruct(shape, kind)

    def run(kernel, operands, results, scratch, block_rows, passes, scalars=1):
        scalar = [pl.BlockSpec(memory_space=pltpu.SMEM)] * scalars
        vector = pl.BlockSpec(memory_space=pltpu.VMEM)
        return pl.pallas_call(
            kernel,
            out_shape=results,
            in_specs=scalar + [vector] * (len(operands) - scalars),
            out_specs=[vector] * len(results),
            scratch_shapes=scratch,
            compiler_params=pltpu.CompilerParams(vmem_limit_bytes=VMEM_LIMIT),
            cost_estimate=pl.CostEstimate(
                flops=block_rows * passes * 2 * rows * lanes * lanes,
                bytes_accessed=block_rows * 6 * lanes * lanes * 2 + 1000000,
                transcendentals=0,
            ),
            name=kernel.__name__,
        )(*operands)

    send_first, send_second = run(
        edge_squares, (state2,), [shaped((2, steps, lanes), bf16)] * 2, [], PREFETCH_ROWS, 6, 0
    )
    first, second = exchange(send_first, send_second, "space")

    outer_in, smooth_in = run(
        source_inside,
        (couple, state2, forcing2, initial, blocks, precond),
        [shaped((width - 4, rows, lanes))] * 2,
        [pltpu.VMEM((width, steps, lanes), bf16)],
        width - 4,
        6,
    )
    outer_ed, smooth_ed, send_first, send_second = run(
        source_edges,
        (couple, first, second, state2, forcing2, initial, blocks, precond),
        [shaped((4, rows, lanes))] * 2 + [shaped((2, rows, lanes), bf16)] * 2,
        [pltpu.VMEM((2, 6, steps, lanes), bf16)],
        4,
        6,
    )
    first, second = exchange(send_first, send_second, "space")
    out_outer, out_inner, out_next = run(
        solve_inside,
        (couple, smooth_in, smooth_ed, outer_in, blocks, precond),
        [shaped(flat), shaped(flat), shaped((2 * width, lanes))],
        [pltpu.VMEM((width, rows, lanes), bf16)],
        width - 4,
        9,
    )
    local, ends = run(
        solve_edges,
        (couple, first, second, smooth_in, smooth_ed, outer_ed, blocks, precond, out_outer, out_inner, out_next, state2),
        [shaped(flat), shaped((GROUP, 2, width, lanes), bf16)],
        [
            pltpu.VMEM((2, 6, rows, lanes), bf16),
            pltpu.VMEM(flat, f32),
            pltpu.VMEM(flat, f32),
            pltpu.VMEM((2 * width, lanes), f32),
        ],
        4,
        9,
    )
    carry = ring_carry(ends, steps)
    (out,) = run(finish_kernel, (local, carry), [shaped(flat)], [], 1, 1, 0)
    return out.reshape(state.shape)


def solution(mesh):
    placed = (
        P("tm", "space", None),
        P("tm", "space", None),
        P("space", None),
        P(None, "space", None, None),
        P("space", None, None),
        P("space", None),
    )
    return jax.shard_map(
        on_device, mesh=mesh, in_specs=placed, out_specs=P("tm", "space", None), check_vma=False
    )
```

```python
import jax
import jax.numpy as jnp
from jax import lax
from jax.experimental import pallas as pl
from jax.experimental.pallas import tpu as pltpu
from jax.sharding import PartitionSpec as P

alpha_rate = 0.5
time_step = 0.5
relaxation = 0.7
GROUP = 16
EXTRA = 16
SLOTS = 5
PREFETCH_ROWS = 400
VMEM_LIMIT = 16 * 1024 * 1024


def times_transposed(x, w):
    return lax.dot_general(x, w, (((1,), (1,)), ((), ())), preferred_element_type=jnp.float32)


def exchange(first_edge, second_edge, axis):
    count = lax.axis_size(axis)
    first, second = [], []
    for i in range(count - 1):
        (first if i & 1 else second).extend([(i, i + 1), (i + 1, i)])
    return lax.ppermute(first_edge, axis, first), lax.ppermute(second_edge, axis, second)


def is_odd():
    return (lax.axis_index("space") & 1) == 1


def fill_windows(windows, first_ref, second_ref, inside, width):
    for k in range(4):
        windows[0, 2 + k] = inside(k)
        windows[1, k] = inside(width - 4 + k)

    @pl.when(is_odd())
    def _():
        windows[0, 0:2] = second_ref[...]
        windows[1, 4:6] = first_ref[...]

    @pl.when(jnp.logical_not(is_odd()))
    def _():
        windows[0, 0:2] = first_ref[...]
        windows[1, 4:6] = second_ref[...]


def squared(state_ref, j, width, steps):
    s = state_ref[pl.ds(j, steps, stride=width), :]
    return (0.5 * s * s).astype(jnp.bfloat16)


def block_residual(j, flux, state_ref, forcing_ref, initial_ref):
    steps, lanes = flux.shape
    width = initial_ref.shape[0]
    position = lax.axis_index("tm")
    s = state_ref[pl.ds(j, steps, stride=width), :]
    f = forcing_ref[pl.ds(j, steps, stride=width), :]
    first = jnp.where(position == 0, initial_ref[pl.ds(j, 1), :], 0.0)
    row = lax.broadcasted_iota(jnp.int32, (steps, lanes), 0)
    previous = jnp.where(row == 0, jnp.broadcast_to(first, s.shape), pltpu.roll(s, 1, 0))
    residual = f - s + previous - time_step * flux
    onward = state_ref[pl.ds((steps - 1) * width + j, 1), :]
    onward = jnp.where(position == lax.axis_size("tm") - 1, 0.0, onward)
    row = lax.broadcasted_iota(jnp.int32, (EXTRA, lanes), 0)
    tail = jnp.where(row == 0, jnp.broadcast_to(onward, (EXTRA, lanes)), 0.0)
    return jnp.concatenate([residual, tail], 0)


def pair_product(x, w):
    rows = x[0].shape[0]
    zero = jnp.zeros_like(x[0])
    left = jnp.concatenate([jnp.concatenate([x[0], zero], 1), jnp.concatenate([zero, x[1]], 1)], 0)
    both = times_transposed(left, jnp.concatenate(w, 1))
    return both[:rows], both[rows:]


def coupled_pair(j, at, picked, couple, blocks_ref):
    deep = SLOTS - 1
    last = pair_product(
        [picked[at + k + couple[deep, j + k]] for k in range(2)],
        [blocks_ref[deep, j + k] for k in range(2)],
    )
    total = []
    for k in range(2):
        rows = jnp.concatenate([picked[at + k + couple[s, j + k]] for s in range(deep)], 1)
        weights = jnp.concatenate([blocks_ref[s, j + k] for s in range(deep)], 1)
        total.append(times_transposed(rows, weights) + last[k])
    return total


def solve_source(j, flux, state_ref, forcing_ref, initial_ref, precond_ref):
    rows = [block_residual(j + k, flux[k], state_ref, forcing_ref, initial_ref) for k in range(2)]
    smooth = pair_product(
        [r.astype(jnp.bfloat16) for r in rows], [precond_ref[j + k] for k in range(2)]
    )
    return [2.0 * rows[k] - relaxation * smooth[k] for k in range(2)], smooth


def edge_squares(state_ref, send_first, send_second):
    _, steps, _ = send_first.shape
    width = state_ref.shape[0] // steps

    @pl.when(is_odd())
    def _():
        for k in range(2):
            send_first[k] = squared(state_ref, width - 2 + k, width, steps)
            send_second[k] = squared(state_ref, k, width, steps)

    @pl.when(jnp.logical_not(is_odd()))
    def _():
        for k in range(2):
            send_first[k] = squared(state_ref, k, width, steps)
            send_second[k] = squared(state_ref, width - 2 + k, width, steps)


def source_inside(couple, state_ref, forcing_ref, initial_ref, blocks_ref, precond_ref, outer_ref, smooth_ref, squares):
    width, steps, _ = squares.shape
    for j in range(width):
        squares[j] = squared(state_ref, j, width, steps)
    ahead = coupled_pair(2, 2, squares, couple, blocks_ref)
    for j in range(2, width - 2, 2):
        flux = ahead
        if j + 2 < width - 2:
            ahead = coupled_pair(j + 2, j + 2, squares, couple, blocks_ref)
        outer, smooth = solve_source(j, flux, state_ref, forcing_ref, initial_ref, precond_ref)
        for k in range(2):
            outer_ref[j - 2 + k] = outer[k]
            smooth_ref[j - 2 + k] = smooth[k]


def source_edges(couple, first_ref, second_ref, state_ref, forcing_ref, initial_ref, blocks_ref, precond_ref, outer_ref, smooth_ref, send_first, send_second, windows):
    width = initial_ref.shape[0]
    steps = windows.shape[2]
    fill_windows(windows, first_ref, second_ref, lambda k: squared(state_ref, k, width, steps), width)
    fluxes = [
        coupled_pair(e * (width - 2), 2, windows.at[e], couple, blocks_ref) for e in range(2)
    ]
    for e in range(2):
        j = e * (width - 2)
        outer, smooth = solve_source(j, fluxes[e], state_ref, forcing_ref, initial_ref, precond_ref)
        for k in range(2):
            outer_ref[2 * e + k] = outer[k]
            smooth_ref[2 * e + k] = smooth[k]

    @pl.when(is_odd())
    def _():
        send_first[...] = smooth_ref[2:4].astype(jnp.bfloat16)
        send_second[...] = smooth_ref[0:2].astype(jnp.bfloat16)

    @pl.when(jnp.logical_not(is_odd()))
    def _():
        send_first[...] = smooth_ref[0:2].astype(jnp.bfloat16)
        send_second[...] = smooth_ref[2:4].astype(jnp.bfloat16)


def split(value):
    high = value.astype(jnp.bfloat16)
    return [high, (value - high.astype(jnp.float32)).astype(jnp.bfloat16)]


def solve_pair(j, coupled, outer, smooth, precond_ref, out_outer, out_inner, out_next, width):
    rows = coupled[0].shape[0]
    steps = rows - EXTRA
    pieces = []
    for k in range(2):
        inner = relaxation * (smooth[k] - time_step * coupled[k])
        pieces.append(jnp.concatenate(split(outer[k]) + split(inner), 0))
    solved = pair_product(pieces, [precond_ref[j + k] for k in range(2)])
    for k in range(2):
        outer_k = solved[k][:rows] + solved[k][rows : 2 * rows]
        inner_k = solved[k][2 * rows : 3 * rows] + solved[k][3 * rows :]
        out_outer[pl.ds(j + k, steps, stride=width), :] = outer_k[:steps]
        out_inner[pl.ds(j + k, steps, stride=width), :] = inner_k[:steps]
        out_next[pl.ds(j + k, 1), :] = outer_k[steps : steps + 1]
        out_next[pl.ds(width + j + k, 1), :] = inner_k[steps : steps + 1]


def solve_inside(couple, all_inside_ref, all_edges_ref, outer_ref, blocks_ref, precond_ref, out_outer, out_inner, out_next, rounded):
    width = rounded.shape[0]
    for k in range(2):
        rounded[k] = all_edges_ref[k].astype(jnp.bfloat16)
        rounded[width - 2 + k] = all_edges_ref[2 + k].astype(jnp.bfloat16)
    for k in range(width - 4):
        rounded[2 + k] = all_inside_ref[k].astype(jnp.bfloat16)
    out_outer[...] = jnp.zeros_like(out_outer)
    out_inner[...] = jnp.zeros_like(out_inner)
    out_next[...] = jnp.zeros_like(out_next)
    ahead = coupled_pair(2, 2, rounded, couple, blocks_ref)
    for j in range(2, width - 2, 2):
        coupled = ahead
        if j + 2 < width - 2:
            ahead = coupled_pair(j + 2, j + 2, rounded, couple, blocks_ref)
        outer = [outer_ref[j - 2 + k] for k in range(2)]
        smooth = [all_inside_ref[j - 2 + k] for k in range(2)]
        solve_pair(j, coupled, outer, smooth, precond_ref, out_outer, out_inner, out_next, width)


def solve_edges(couple, first_ref, second_ref, all_inside_ref, all_edges_ref, outer_ref, blocks_ref, precond_ref, in_outer, in_inner, in_next, state_ref, result_ref, ends_ref, windows, my_outer, my_inner, my_next):
    width = in_next.shape[0] // 2
    steps = in_outer.shape[0] // width

    def inside(k):
        if k < 2:
            return all_edges_ref[k].astype(jnp.bfloat16)
        if k >= width - 2:
            return all_edges_ref[k - width + 4].astype(jnp.bfloat16)
        return all_inside_ref[k - 2].astype(jnp.bfloat16)

    fill_windows(windows, first_ref, second_ref, inside, width)
    my_outer[...] = in_outer[...]
    my_inner[...] = in_inner[...]
    my_next[...] = in_next[...]
    coupled = [
        coupled_pair(e * (width - 2), 2, windows.at[e], couple, blocks_ref) for e in range(2)
    ]
    for e in range(2):
        j = e * (width - 2)
        outer = [outer_ref[2 * e + k] for k in range(2)]
        smooth = [all_edges_ref[2 * e + k] for k in range(2)]
        solve_pair(j, coupled[e], outer, smooth, precond_ref, my_outer, my_inner, my_next, width)
    z = jnp.zeros((width, 128), jnp.float32)
    y = jnp.zeros((width, 128), jnp.float32)
    for n in range(steps):
        rows = pl.ds(n * width, width)
        z = 0.5 * (my_inner[rows, :] + z)
        y = 0.5 * (my_outer[rows, :] + z + y)
        result_ref[rows, :] = state_ref[rows, :] + relaxation * y
    ends_outer = (y + my_next[pl.ds(0, width), :]).astype(jnp.bfloat16)
    ends_inner = (z + my_next[pl.ds(width, width), :]).astype(jnp.bfloat16)
    for k in range(ends_ref.shape[0]):
        ends_ref[k, 0] = ends_outer
        ends_ref[k, 1] = ends_inner


def finish_kernel(local_ref, carry_ref, out_ref):
    width = carry_ref.shape[1]
    steps = out_ref.shape[0] // width
    for n in range(steps):
        rows = pl.ds(n * width, width)
        scale = relaxation * 0.5 ** (n + 1)
        out_ref[rows, :] = local_ref[rows, :] + scale * (carry_ref[0] + (0.5 * (n + 1)) * carry_ref[1])


def carried(power, steps, value):
    scale = jnp.exp2(-float(steps) * power)
    return jnp.stack([scale * value[0] + scale * (0.5 * steps) * power * value[1], scale * value[1]])


def ring_carry(sent, steps):
    count = lax.axis_size("tm")
    position = lax.axis_index("tm")
    groups = count // GROUP
    members = [[g * GROUP + i for i in range(GROUP)] for g in range(groups)]
    mine = position % GROUP
    group = position // GROUP
    got = lax.all_to_all(sent, "tm", 0, 0, axis_index_groups=members, tiled=True)
    got = got.astype(jnp.float32)
    total = jnp.zeros(got.shape[1:], jnp.float32)
    before = total
    for i in range(GROUP):
        total = total + carried(jnp.float32(GROUP - 1 - i), steps, got[i])
        power = (mine - 1 - i).astype(jnp.float32)
        part = carried(jnp.maximum(power, 0.0), steps, got[i])
        before = before + jnp.where(power >= 0, part, 0.0)
    total = total.astype(jnp.bfloat16)
    into = jnp.zeros(got.shape[1:], jnp.float32)
    for m in range(1, groups + 1):
        other = total
        if m < groups:
            route = [(i, (i + m * GROUP) % count) for i in range(count)]
            other = lax.ppermute(total, "tm", route)
        wrapped = jnp.where(m > group, alpha_rate, 1.0)
        power = jnp.float32(GROUP * (m - 1))
        into = into + wrapped * carried(power, steps, other.astype(jnp.float32))
    closing = 1.0 / (1.0 - alpha_rate * 2.0 ** (-steps * count))
    return before + carried(mine.astype(jnp.float32), steps, closing * into)


def on_device(state, forcing, initial, blocks, precond, couple):
    steps, width, lanes = state.shape
    rows = steps + EXTRA
    flat = (steps * width, lanes)
    state2 = state.reshape(flat)
    forcing2 = forcing.reshape(flat)
    couple = couple.T
    f32, bf16 = jnp.float32, jnp.bfloat16

    def shaped(shape, kind=f32):
        return jax.ShapeDtypeStruct(shape, kind)

    def run(kernel, operands, results, scratch, block_rows, passes, scalars=1):
        scalar = [pl.BlockSpec(memory_space=pltpu.SMEM)] * scalars
        vector = pl.BlockSpec(memory_space=pltpu.VMEM)
        return pl.pallas_call(
            kernel,
            out_shape=results,
            in_specs=scalar + [vector] * (len(operands) - scalars),
            out_specs=[vector] * len(results),
            scratch_shapes=scratch,
            compiler_params=pltpu.CompilerParams(vmem_limit_bytes=VMEM_LIMIT),
            cost_estimate=pl.CostEstimate(
                flops=block_rows * passes * 2 * rows * lanes * lanes,
                bytes_accessed=block_rows * 6 * lanes * lanes * 2 + 1000000,
                transcendentals=0,
            ),
            name=kernel.__name__,
        )(*operands)

    send_first, send_second = run(
        edge_squares, (state2,), [shaped((2, steps, lanes), bf16)] * 2, [], PREFETCH_ROWS, 6, 0
    )
    first, second = exchange(send_first, send_second, "space")

    outer_in, smooth_in = run(
        source_inside,
        (couple, state2, forcing2, initial, blocks, precond),
        [shaped((width - 4, rows, lanes))] * 2,
        [pltpu.VMEM((width, steps, lanes), bf16)],
        width - 4,
        6,
    )
    outer_ed, smooth_ed, send_first, send_second = run(
        source_edges,
        (couple, first, second, state2, forcing2, initial, blocks, precond),
        [shaped((4, rows, lanes))] * 2 + [shaped((2, rows, lanes), bf16)] * 2,
        [pltpu.VMEM((2, 6, steps, lanes), bf16)],
        4,
        6,
    )
    first, second = exchange(send_first, send_second, "space")
    out_outer, out_inner, out_next = run(
        solve_inside,
        (couple, smooth_in, smooth_ed, outer_in, blocks, precond),
        [shaped(flat), shaped(flat), shaped((2 * width, lanes))],
        [pltpu.VMEM((width, rows, lanes), bf16)],
        width - 4,
        9,
    )
    local, ends = run(
        solve_edges,
        (couple, first, second, smooth_in, smooth_ed, outer_ed, blocks, precond, out_outer, out_inner, out_next, state2),
        [shaped(flat), shaped((GROUP, 2, width, lanes), bf16)],
        [
            pltpu.VMEM((2, 6, rows, lanes), bf16),
            pltpu.VMEM(flat, f32),
            pltpu.VMEM(flat, f32),
            pltpu.VMEM((2 * width, lanes), f32),
        ],
        4,
        9,
    )
    carry = ring_carry(ends, steps)
    (out,) = run(finish_kernel, (local, carry), [shaped(flat)], [], 1, 1, 0)
    return out.reshape(state.shape)


def solution(mesh):
    placed = (
        P("tm", "space", None),
        P("tm", "space", None),
        P("space", None),
        P(None, "space", None, None),
        P("space", None, None),
        P("space", None),
    )
    return jax.shard_map(
        on_device, mesh=mesh, in_specs=placed, out_specs=P("tm", "space", None), check_vma=False
    )
```

```python
import jax
import jax.numpy as jnp
from jax import lax
from jax.experimental import pallas as pl
from jax.experimental.pallas import tpu as pltpu
from jax.sharding import PartitionSpec as P

alpha_rate = 0.5
time_step = 0.5
relaxation = 0.7
GROUP = 16
EXTRA = 16
SLOTS = 5
PREFETCH_ROWS = 400
VMEM_LIMIT = 16 * 1024 * 1024


def times_transposed(x, w):
    return lax.dot_general(x, w, (((1,), (1,)), ((), ())), preferred_element_type=jnp.float32)


def exchange(first_edge, second_edge, axis):
    count = lax.axis_size(axis)
    first, second = [], []
    for i in range(count - 1):
        (first if i & 1 else second).extend([(i, i + 1), (i + 1, i)])
    return lax.ppermute(first_edge, axis, first), lax.ppermute(second_edge, axis, second)


def is_odd():
    return (lax.axis_index("space") & 1) == 1


def fill_windows(windows, first_ref, second_ref, inside, width):
    for k in range(4):
        windows[0, 2 + k] = inside(k)
        windows[1, k] = inside(width - 4 + k)

    @pl.when(is_odd())
    def _():
        windows[0, 0:2] = second_ref[...]
        windows[1, 4:6] = first_ref[...]

    @pl.when(jnp.logical_not(is_odd()))
    def _():
        windows[0, 0:2] = first_ref[...]
        windows[1, 4:6] = second_ref[...]


def squared(state_ref, j, width, steps):
    s = state_ref[pl.ds(j, steps, stride=width), :]
    return (0.5 * s * s).astype(jnp.bfloat16)


def block_residual(j, flux, state_ref, forcing_ref, initial_ref):
    steps, lanes = flux.shape
    width = initial_ref.shape[0]
    position = lax.axis_index("tm")
    s = state_ref[pl.ds(j, steps, stride=width), :]
    f = forcing_ref[pl.ds(j, steps, stride=width), :]
    first = jnp.where(position == 0, initial_ref[pl.ds(j, 1), :], 0.0)
    row = lax.broadcasted_iota(jnp.int32, (steps, lanes), 0)
    previous = jnp.where(row == 0, jnp.broadcast_to(first, s.shape), pltpu.roll(s, 1, 0))
    residual = f - s + previous - time_step * flux
    onward = state_ref[pl.ds((steps - 1) * width + j, 1), :]
    onward = jnp.where(position == lax.axis_size("tm") - 1, 0.0, onward)
    row = lax.broadcasted_iota(jnp.int32, (EXTRA, lanes), 0)
    tail = jnp.where(row == 0, jnp.broadcast_to(onward, (EXTRA, lanes)), 0.0)
    return jnp.concatenate([residual, tail], 0)


def pair_product(x, w):
    rows = x[0].shape[0]
    zero = jnp.zeros_like(x[0])
    left = jnp.concatenate([jnp.concatenate([x[0], zero], 1), jnp.concatenate([zero, x[1]], 1)], 0)
    both = times_transposed(left, jnp.concatenate(w, 1))
    return both[:rows], both[rows:]


def coupled_pair(j, at, picked, couple, blocks_ref):
    deep = SLOTS - 1
    last = pair_product(
        [picked[at + k + couple[deep, j + k]] for k in range(2)],
        [blocks_ref[deep, j + k] for k in range(2)],
    )
    total = []
    for k in range(2):
        rows = jnp.concatenate([picked[at + k + couple[s, j + k]] for s in range(deep)], 1)
        weights = jnp.concatenate([blocks_ref[s, j + k] for s in range(deep)], 1)
        total.append(times_transposed(rows, weights) + last[k])
    return total


def solve_source(j, flux, state_ref, forcing_ref, initial_ref, precond_ref):
    rows = [block_residual(j + k, flux[k], state_ref, forcing_ref, initial_ref) for k in range(2)]
    smooth = pair_product(
        [r.astype(jnp.bfloat16) for r in rows], [precond_ref[j + k] for k in range(2)]
    )
    return [2.0 * rows[k] - relaxation * smooth[k] for k in range(2)], smooth


def edge_squares(state_ref, send_first, send_second):
    _, steps, _ = send_first.shape
    width = state_ref.shape[0] // steps

    @pl.when(is_odd())
    def _():
        for k in range(2):
            send_first[k] = squared(state_ref, width - 2 + k, width, steps)
            send_second[k] = squared(state_ref, k, width, steps)

    @pl.when(jnp.logical_not(is_odd()))
    def _():
        for k in range(2):
            send_first[k] = squared(state_ref, k, width, steps)
            send_second[k] = squared(state_ref, width - 2 + k, width, steps)


def source_inside(couple, state_ref, forcing_ref, initial_ref, blocks_ref, precond_ref, outer_ref, smooth_ref, squares):
    width, steps, _ = squares.shape
    for j in range(width):
        squares[j] = squared(state_ref, j, width, steps)
    ahead = coupled_pair(2, 2, squares, couple, blocks_ref)
    for j in range(2, width - 2, 2):
        flux = ahead
        if j + 2 < width - 2:
            ahead = coupled_pair(j + 2, j + 2, squares, couple, blocks_ref)
        outer, smooth = solve_source(j, flux, state_ref, forcing_ref, initial_ref, precond_ref)
        for k in range(2):
            outer_ref[j - 2 + k] = outer[k]
            smooth_ref[j - 2 + k] = smooth[k]


def source_edges(couple, first_ref, second_ref, state_ref, forcing_ref, initial_ref, blocks_ref, precond_ref, outer_ref, smooth_ref, send_first, send_second, windows):
    width = initial_ref.shape[0]
    steps = windows.shape[2]
    fill_windows(windows, first_ref, second_ref, lambda k: squared(state_ref, k, width, steps), width)
    fluxes = [
        coupled_pair(e * (width - 2), 2, windows.at[e], couple, blocks_ref) for e in range(2)
    ]
    for e in range(2):
        j = e * (width - 2)
        outer, smooth = solve_source(j, fluxes[e], state_ref, forcing_ref, initial_ref, precond_ref)
        for k in range(2):
            outer_ref[2 * e + k] = outer[k]
            smooth_ref[2 * e + k] = smooth[k]

    @pl.when(is_odd())
    def _():
        send_first[...] = smooth_ref[2:4].astype(jnp.bfloat16)
        send_second[...] = smooth_ref[0:2].astype(jnp.bfloat16)

    @pl.when(jnp.logical_not(is_odd()))
    def _():
        send_first[...] = smooth_ref[0:2].astype(jnp.bfloat16)
        send_second[...] = smooth_ref[2:4].astype(jnp.bfloat16)


def split(value):
    high = value.astype(jnp.bfloat16)
    return [high, (value - high.astype(jnp.float32)).astype(jnp.bfloat16)]


def solve_pair(j, coupled, outer, smooth, precond_ref, out_outer, out_inner, out_next, width):
    rows = coupled[0].shape[0]
    steps = rows - EXTRA
    pieces = []
    for k in range(2):
        inner = relaxation * (smooth[k] - time_step * coupled[k])
        pieces.append(jnp.concatenate(split(outer[k]) + split(inner), 0))
    solved = pair_product(pieces, [precond_ref[j + k] for k in range(2)])
    for k in range(2):
        outer_k = solved[k][:rows] + solved[k][rows : 2 * rows]
        inner_k = solved[k][2 * rows : 3 * rows] + solved[k][3 * rows :]
        out_outer[pl.ds(j + k, steps, stride=width), :] = outer_k[:steps]
        out_inner[pl.ds(j + k, steps, stride=width), :] = inner_k[:steps]
        out_next[pl.ds(j + k, 1), :] = outer_k[steps : steps + 1]
        out_next[pl.ds(width + j + k, 1), :] = inner_k[steps : steps + 1]


def solve_inside(couple, all_inside_ref, all_edges_ref, outer_ref, blocks_ref, precond_ref, out_outer, out_inner, out_next, rounded):
    width = rounded.shape[0]
    for k in range(2):
        rounded[k] = all_edges_ref[k].astype(jnp.bfloat16)
        rounded[width - 2 + k] = all_edges_ref[2 + k].astype(jnp.bfloat16)
    for k in range(width - 4):
        rounded[2 + k] = all_inside_ref[k].astype(jnp.bfloat16)
    out_outer[...] = jnp.zeros_like(out_outer)
    out_inner[...] = jnp.zeros_like(out_inner)
    out_next[...] = jnp.zeros_like(out_next)
    ahead = coupled_pair(2, 2, rounded, couple, blocks_ref)
    for j in range(2, width - 2, 2):
        coupled = ahead
        if j + 2 < width - 2:
            ahead = coupled_pair(j + 2, j + 2, rounded, couple, blocks_ref)
        outer = [outer_ref[j - 2 + k] for k in range(2)]
        smooth = [all_inside_ref[j - 2 + k] for k in range(2)]
        solve_pair(j, coupled, outer, smooth, precond_ref, out_outer, out_inner, out_next, width)


def solve_edges(couple, first_ref, second_ref, all_inside_ref, all_edges_ref, outer_ref, blocks_ref, precond_ref, in_outer, in_inner, in_next, state_ref, result_ref, ends_ref, windows, my_outer, my_inner, my_next):
    width = in_next.shape[0] // 2
    steps = in_outer.shape[0] // width

    def inside(k):
        if k < 2:
            return all_edges_ref[k].astype(jnp.bfloat16)
        if k >= width - 2:
            return all_edges_ref[k - width + 4].astype(jnp.bfloat16)
        return all_inside_ref[k - 2].astype(jnp.bfloat16)

    fill_windows(windows, first_ref, second_ref, inside, width)
    for n in range(steps):
        for start in (0, width - 8):
            rows = pl.ds(n * width + start, 8)
            my_outer[rows, :] = in_outer[rows, :]
            my_inner[rows, :] = in_inner[rows, :]
    my_next[...] = in_next[...]
    coupled = [
        coupled_pair(e * (width - 2), 2, windows.at[e], couple, blocks_ref) for e in range(2)
    ]
    for e in range(2):
        j = e * (width - 2)
        outer = [outer_ref[2 * e + k] for k in range(2)]
        smooth = [all_edges_ref[2 * e + k] for k in range(2)]
        solve_pair(j, coupled[e], outer, smooth, precond_ref, my_outer, my_inner, my_next, width)
    z = jnp.zeros((width, 128), jnp.float32)
    y = jnp.zeros((width, 128), jnp.float32)
    for n in range(steps):
        rows = pl.ds(n * width, width)
        low, middle, high = pl.ds(n * width, 8), pl.ds(n * width + 8, width - 16), pl.ds((n + 1) * width - 8, 8)
        inner = jnp.concatenate([my_inner[low, :], in_inner[middle, :], my_inner[high, :]], 0)
        outer = jnp.concatenate([my_outer[low, :], in_outer[middle, :], my_outer[high, :]], 0)
        z = 0.5 * (inner + z)
        y = 0.5 * (outer + z + y)
        result_ref[rows, :] = state_ref[rows, :] + relaxation * y
    ends_outer = (y + my_next[pl.ds(0, width), :]).astype(jnp.bfloat16)
    ends_inner = (z + my_next[pl.ds(width, width), :]).astype(jnp.bfloat16)
    for k in range(ends_ref.shape[0]):
        ends_ref[k, 0] = ends_outer
        ends_ref[k, 1] = ends_inner


def finish_kernel(local_ref, carry_ref, out_ref):
    width = carry_ref.shape[1]
    steps = out_ref.shape[0] // width
    for n in range(steps):
        rows = pl.ds(n * width, width)
        scale = relaxation * 0.5 ** (n + 1)
        out_ref[rows, :] = local_ref[rows, :] + scale * (carry_ref[0] + (0.5 * (n + 1)) * carry_ref[1])


def carried(power, steps, value):
    scale = jnp.exp2(-float(steps) * power)
    return jnp.stack([scale * value[0] + scale * (0.5 * steps) * power * value[1], scale * value[1]])


def ring_carry(sent, steps):
    count = lax.axis_size("tm")
    position = lax.axis_index("tm")
    groups = count // GROUP
    members = [[g * GROUP + i for i in range(GROUP)] for g in range(groups)]
    mine = position % GROUP
    group = position // GROUP
    got = lax.all_to_all(sent, "tm", 0, 0, axis_index_groups=members, tiled=True)
    got = got.astype(jnp.float32)
    total = jnp.zeros(got.shape[1:], jnp.float32)
    before = total
    for i in range(GROUP):
        total = total + carried(jnp.float32(GROUP - 1 - i), steps, got[i])
        power = (mine - 1 - i).astype(jnp.float32)
        part = carried(jnp.maximum(power, 0.0), steps, got[i])
        before = before + jnp.where(power >= 0, part, 0.0)
    total = total.astype(jnp.bfloat16)
    into = jnp.zeros(got.shape[1:], jnp.float32)
    for m in range(1, groups + 1):
        other = total
        if m < groups:
            route = [(i, (i + m * GROUP) % count) for i in range(count)]
            other = lax.ppermute(total, "tm", route)
        wrapped = jnp.where(m > group, alpha_rate, 1.0)
        power = jnp.float32(GROUP * (m - 1))
        into = into + wrapped * carried(power, steps, other.astype(jnp.float32))
    closing = 1.0 / (1.0 - alpha_rate * 2.0 ** (-steps * count))
    return before + carried(mine.astype(jnp.float32), steps, closing * into)


def on_device(state, forcing, initial, blocks, precond, couple):
    steps, width, lanes = state.shape
    rows = steps + EXTRA
    flat = (steps * width, lanes)
    state2 = state.reshape(flat)
    forcing2 = forcing.reshape(flat)
    couple = couple.T
    f32, bf16 = jnp.float32, jnp.bfloat16

    def shaped(shape, kind=f32):
        return jax.ShapeDtypeStruct(shape, kind)

    def run(kernel, operands, results, scratch, block_rows, passes, scalars=1):
        scalar = [pl.BlockSpec(memory_space=pltpu.SMEM)] * scalars
        vector = pl.BlockSpec(memory_space=pltpu.VMEM)
        return pl.pallas_call(
            kernel,
            out_shape=results,
            in_specs=scalar + [vector] * (len(operands) - scalars),
            out_specs=[vector] * len(results),
            scratch_shapes=scratch,
            compiler_params=pltpu.CompilerParams(vmem_limit_bytes=VMEM_LIMIT),
            cost_estimate=pl.CostEstimate(
                flops=block_rows * passes * 2 * rows * lanes * lanes,
                bytes_accessed=block_rows * 6 * lanes * lanes * 2 + 1000000,
                transcendentals=0,
            ),
            name=kernel.__name__,
        )(*operands)

    send_first, send_second = run(
        edge_squares, (state2,), [shaped((2, steps, lanes), bf16)] * 2, [], PREFETCH_ROWS, 6, 0
    )
    first, second = exchange(send_first, send_second, "space")

    outer_in, smooth_in = run(
        source_inside,
        (couple, state2, forcing2, initial, blocks, precond),
        [shaped((width - 4, rows, lanes))] * 2,
        [pltpu.VMEM((width, steps, lanes), bf16)],
        width - 4,
        6,
    )
    outer_ed, smooth_ed, send_first, send_second = run(
        source_edges,
        (couple, first, second, state2, forcing2, initial, blocks, precond),
        [shaped((4, rows, lanes))] * 2 + [shaped((2, rows, lanes), bf16)] * 2,
        [pltpu.VMEM((2, 6, steps, lanes), bf16)],
        4,
        6,
    )
    first, second = exchange(send_first, send_second, "space")
    out_outer, out_inner, out_next = run(
        solve_inside,
        (couple, smooth_in, smooth_ed, outer_in, blocks, precond),
        [shaped(flat), shaped(flat), shaped((2 * width, lanes))],
        [pltpu.VMEM((width, rows, lanes), bf16)],
        width - 4,
        9,
    )
    local, ends = run(
        solve_edges,
        (couple, first, second, smooth_in, smooth_ed, outer_ed, blocks, precond, out_outer, out_inner, out_next, state2),
        [shaped(flat), shaped((GROUP, 2, width, lanes), bf16)],
        [
            pltpu.VMEM((2, 6, rows, lanes), bf16),
            pltpu.VMEM(flat, f32),
            pltpu.VMEM(flat, f32),
            pltpu.VMEM((2 * width, lanes), f32),
        ],
        4,
        9,
    )
    carry = ring_carry(ends, steps)
    (out,) = run(finish_kernel, (local, carry), [shaped(flat)], [], 1, 1, 0)
    return out.reshape(state.shape)


def solution(mesh):
    placed = (
        P("tm", "space", None),
        P("tm", "space", None),
        P("space", None),
        P(None, "space", None, None),
        P("space", None, None),
        P("space", None),
    )
    return jax.shard_map(
        on_device, mesh=mesh, in_specs=placed, out_specs=P("tm", "space", None), check_vma=False
    )
```
